32 devices in a mesh: groups: 2 (over y), track: 4 (over z), across: 2 (over x), disp: 2 (over core).
Axes of the slice: x: 2, y: 2, z: 4, core: 2. Of those that a mesh axis runs over, the one named last changes fastest.
Arguments:
- ref_image: bfloat16 [128, 512], P(('groups', 'across'), 'track'), parts along dimension 0, may hold values from -8 to 8
- source_one: bfloat16 [128, 512], P(('groups', 'across'), 'track'), parts along dimension 0, may hold values from -8 to 8
- source_two: bfloat16 [128, 512], P(('groups', 'across'), 'track'), parts along dimension 0, may hold values from -8 to 8
- plane_offsets: int32 [256], P('disp'), may hold values from 0 to 319, as said below
- intersection_mask: int32 [2, 4, 4], P(None, ('groups', 'across'), 'track'), parts along dimension 1, may hold values 0 or 1
Outputs:
- disparity_map: float32 [128, 512], P(('groups', 'across'), 'track'), parts along dimension 0
- soft_cost: float32 [128, 512], P(('groups', 'across'), 'track'), parts along dimension 0
The draws below stay inside these ranges and needn't reach their ends.
There are 2 independent parts, one for each index of `groups`. The reference program is written for one: setup_inputs(seed, part) draws one part's arguments, and reference() takes and returns one part's arrays. A program takes and returns all parts, laid end to end along the dimension named above; an argument that names none is the same for every part. Nothing has to cross between parts.
Inputs may be any that keep to these rules, and one draw needn't show every extreme that they name: `plane_offsets`: distinct and increasing; the first is 0 and the last is 319.
All inputs are finite; a program needn't handle non-finite values. No bound on the sum of `intersection_mask` on one device may be relied on, other than what follows from the above.
Results may differ from the reference program's by a relative error of at most 0.0003.
Values may be sent and summed in bfloat16 or wider, within the bound.
A program may use at most 64 MiB of HBM per device.

```python
import jax
import jax.numpy as jnp
from jax import lax

PLANES = 256
MAXD = 320
RADIUS = 15
TW = 32
TH = 128
TILES_ACROSS = 2
TILES_TRACK = 4
NA = 64
NT = 512


def texture(key, salt):
    noise_key = jax.random.fold_in(key, salt)
    values = jnp.clip(jax.random.normal(noise_key, (NA, NT), jnp.float32), -4.0, 4.0)
    return values.astype(jnp.bfloat16)


def draw_ref_image(key, part):
    return texture(key, 11)


def draw_source_one(key, part):
    return texture(key, 12)


def draw_source_two(key, part):
    return texture(key, 13)


def draw_plane_offsets(key, part):
    inner = jax.random.permutation(jax.random.fold_in(key, 29), MAXD - 2)[:PLANES - 2].astype(jnp.int32) + 1
    return jnp.concatenate([jnp.zeros((1,), jnp.int32), jnp.sort(inner), jnp.full((1,), MAXD - 1, jnp.int32)])


def plant(entries, stream_key, low, top_value):
    shape = entries.shape
    place = [jax.random.randint(jax.random.fold_in(stream_key, axis), (), 0, shape[axis]) for axis in range(len(shape))]
    entries = entries.at[tuple(place)].set(low)
    longest = shape.index(max(shape))
    place[longest] = (place[longest] + 1) % shape[longest]
    return entries.at[tuple(place)].set(top_value)


def setup_inputs(seed: int = 0, part: int = 0) -> dict:
    streams_of = jax.random.split(jax.random.key(seed), 6)
    own_keys = jax.random.split(jax.random.fold_in(streams_of[5], part), 6)
    ref_image = draw_ref_image(jax.random.fold_in(jax.random.fold_in(streams_of[5], part), 71), part)
    source_one = draw_source_one(jax.random.fold_in(jax.random.fold_in(streams_of[5], part), 71), part)
    source_two = draw_source_two(jax.random.fold_in(jax.random.fold_in(streams_of[5], part), 71), part)
    plane_offsets = draw_plane_offsets(jax.random.fold_in(streams_of[5], 71), part)
    intersection_mask = plant((jax.random.randint(own_keys[4], (2, TILES_ACROSS, TILES_TRACK), 0, 3) < 2).astype(jnp.int32), jax.random.fold_in(own_keys[4], 1), 0, 1)
    return dict(ref_image=ref_image, source_one=source_one, source_two=source_two, plane_offsets=plane_offsets, intersection_mask=intersection_mask)


clip_level = 2.0
exponent_sharpness = 0.005
disparity_interval = 64.0


def window_count(length):
    position = jnp.arange(length, dtype=jnp.int32)
    upper_part = jnp.minimum(position + RADIUS, length - 1)
    lower_part = jnp.maximum(position - RADIUS, 0)
    return (upper_part - lower_part + 1).astype(jnp.float32)


def window_sum(values, along):
    length = values.shape[along]
    widths = [(0, 0), (0, 0)]
    widths[along] = (RADIUS + 1, RADIUS)
    running = jnp.cumsum(jnp.pad(values, widths), axis=along)
    upper_part = lax.slice_in_dim(running, 2 * RADIUS + 1, 2 * RADIUS + 1 + length, axis=along)
    lower_part = lax.slice_in_dim(running, 0, length, axis=along)
    return upper_part - lower_part


def reference(ref_image, source_one, source_two, plane_offsets, intersection_mask):
    total_cols, total_rows = ref_image.shape
    base_image = ref_image.astype(jnp.float32)
    sources = jnp.stack([source_one, source_two]).astype(jnp.float32)
    cell_count = window_count(total_cols)[:, None] * window_count(total_rows)[None, :]
    weights = jnp.repeat(jnp.repeat(intersection_mask.astype(jnp.float32), TW, axis=1), TH, axis=2)
    mask_total = jnp.maximum(weights[0] + weights[1], 1.0)
    row_index = jnp.arange(total_rows, dtype=jnp.int32)

    def aggregate(frame_index, offset_rows):
        source_rows = row_index - offset_rows
        in_strip = source_rows >= 0
        sampled = jnp.take(sources[frame_index], jnp.clip(source_rows, 0, total_rows - 1), axis=1)
        term_cost = jnp.where(in_strip[None, :], jnp.minimum(jnp.abs(base_image - sampled), clip_level), clip_level)
        return window_sum(window_sum(term_cost - 1.0, 1), 0) / cell_count + 1.0

    def plane_step(running, offset):
        maximal_matching_likelihood, normalizer_mass, disparity_moment_accumulator = running
        hypothesis_matching_penalty = (weights[0] * aggregate(0, offset) + weights[1] * aggregate(1, 2 * offset)) / mask_total
        hypothesis_likelihoods = -hypothesis_matching_penalty / exponent_sharpness
        new_top = jnp.maximum(maximal_matching_likelihood, hypothesis_likelihoods)
        fading = jnp.exp(maximal_matching_likelihood - new_top)
        lifted = jnp.exp(hypothesis_likelihoods - new_top)
        return (new_top, normalizer_mass * fading + lifted, disparity_moment_accumulator * fading + lifted * offset.astype(jnp.float32)), None

    initial = jnp.full(base_image.shape, -jnp.inf, jnp.float32)
    blank_map = jnp.zeros(base_image.shape, jnp.float32)
    (maximal_matching_likelihood, normalizer_mass, disparity_moment_accumulator), _ = lax.scan(plane_step, (initial, blank_map, blank_map), plane_offsets)
    return disparity_moment_accumulator / normalizer_mass / disparity_interval, -exponent_sharpness * (maximal_matching_likelihood + jnp.log(normalizer_mass))
```

```python
import functools

import jax
import jax.numpy as jnp
from jax import lax
from jax.experimental import pallas as pl
from jax.experimental.pallas import tpu as pltpu
from jax.sharding import PartitionSpec as P

MAXD = 320
RADIUS = 15
HALO = RADIUS + 1
CLIP = 2.0
SHARPNESS = 0.005
INTERVAL = 64.0
BIG = 1e30
GROUP = 4
BATCH = 4


def kernel(
    sizes, offs, mask, r_ref, s1_ref, s2_ref, disp_out, soft_out,
    rx, window, refs, weights, terms, box, scores, top, tx, mrx,
    send_sem, recv_sem, msend, mrecv,
):
    track, across, disp, cols, rows, planes = sizes
    ext = cols + 2 * HALO
    wide = 2 * ext
    span = rows + 2 * HALO
    deep = -(-(2 * (MAXD - 1) + RADIUS) // rows)
    deep0 = -(-(MAXD - 1 + RADIUS) // rows)
    back = min(deep, track - 1)
    ahead = back + 1
    r = lax.axis_index("track")
    c = lax.axis_index("across")
    d = lax.axis_index("disp")
    images = (s1_ref, s2_ref, r_ref)

    def present(dr, dc):
        return (r + dr >= 0) & (r + dr < track) & (c + dc >= 0) & (c + dc < across)

    barrier = pltpu.get_barrier_semaphore()
    for dr in range(-back, back + 1):
        for dc in (-1, 0, 1):
            if dr == 0 and dc == 0:
                continue

            @pl.when(present(dr, dc))
            def _():
                pl.semaphore_signal(barrier, inc=1, device_id={"track": r + dr, "across": c + dc})

    for i in range(1, disp):
        pl.semaphore_signal(barrier, inc=1, device_id={"disp": lax.rem(d + i, disp)})
    n_rows = jnp.minimum(r, back) + jnp.minimum(track - 1 - r, back) + 1
    n_cols = jnp.minimum(c, 1) + jnp.minimum(across - 1 - c, 1) + 1
    pl.semaphore_wait(barrier, n_rows * n_cols - 1 + disp - 1)

    def needed(slot):
        if slot == ahead:
            return (0, 1, 2)
        if slot <= 1:
            return (0, 1, 2)
        return (0, 1) if slot <= deep0 else (1,)

    def shift_of(slot):
        return -1 if slot == ahead else slot

    def copy(slot, image, dc):
        if dc == 0:
            src, lo, n = images[image], HALO, cols
        elif dc == 1:
            src, lo, n = images[image].at[pl.ds(cols - HALO, HALO)], 0, HALO
        else:
            src, lo, n = images[image].at[pl.ds(0, HALO)], HALO + cols, HALO
        return pltpu.make_async_remote_copy(
            src_ref=src,
            dst_ref=rx.at[slot, image, pl.ds(lo, n)],
            send_sem=send_sem.at[slot, image, dc + 1],
            recv_sem=recv_sem.at[slot, image, dc + 1],
            device_id={"track": r + shift_of(slot), "across": c + dc},
        )

    def each_copy(slot):
        for dc in (-1, 0, 1):
            if shift_of(slot) == 0 and dc == 0:
                continue
            yield dc, needed(slot)

    for slot in list(range(back, -1, -1)) + [ahead]:
        for dc, imgs in each_copy(slot):

            @pl.when(present(shift_of(slot), dc))
            def _():
                for image in imgs:
                    copy(slot, image, dc).start()

    for i in range(3):
        rx[0, i, HALO : HALO + cols, :] = images[i][...]
    for slot in range(back + 2):
        for lo, edge in ((0, c == 0), (HALO + cols, c == across - 1)):

            @pl.when(edge)
            def _():
                for i in range(3):
                    rx[slot, i, lo : lo + HALO, :] = jnp.zeros((HALO, rows), jnp.bfloat16)

    for j in range(1, deep + 1):

        @pl.when(r - j < 0)
        def _():
            window[(deep - j) * rows : (deep - j + 1) * rows, :] = jnp.full((rows, wide), BIG, jnp.float32)

    for slot in range(deep0 + 1, back + 1):
        rx[slot, 0] = jnp.zeros((ext, rows), jnp.bfloat16)

    @pl.when(r == 0)
    def _():
        refs[0:HALO, :] = jnp.zeros((HALO, wide), jnp.float32)

    @pl.when(r == track - 1)
    def _():
        refs[HALO + rows :, :] = jnp.zeros((HALO, wide), jnp.float32)
        window[(deep + 1) * rows :, :] = jnp.zeros((HALO, wide), jnp.float32)

    w0 = mask[0, 0, 0].astype(jnp.float32)
    w1 = mask[1, 0, 0].astype(jnp.float32)
    share = jnp.where(w0 + w1 > 1.5, 0.5, 1.0)
    w0, w1 = w0 * share, w1 * share
    lanes = GROUP * cols
    k_lane = lax.broadcasted_iota(jnp.int32, (wide, lanes), 0)
    n_lane = lax.broadcasted_iota(jnp.int32, (wide, lanes), 1)
    column = k_lane % ext - HALO
    gcol = column + c * cols
    near = (
        (jnp.abs(column - n_lane % cols) <= RADIUS) & (gcol >= 0) & (gcol < across * cols)
    )
    frame_weight = jnp.where(near, jnp.where(k_lane < ext, w0, w1), 0.0)
    for q in range(GROUP):
        part = jnp.where(n_lane // cols == q, frame_weight, 0.0).astype(jnp.bfloat16)
        for half in range(2):
            lo = (2 * q + half) * wide
            weights[lo : lo + wide, :] = part

    def arrive(slot):
        for dc, imgs in each_copy(slot):

            @pl.when(present(-shift_of(slot), -dc))
            def _():
                for image in imgs:
                    copy(slot, image, dc).wait_recv()

    def sources(slot):
        both = rx[slot, 0:2].reshape(wide, rows).astype(jnp.float32)
        return both.T

    def reference_rows(slot):
        one = rx[slot, 2].astype(jnp.float32)
        return jnp.concatenate([one, one], axis=0).T

    arrive(0)
    window[deep * rows : (deep + 1) * rows, :] = sources(0)
    refs[HALO : HALO + rows, :] = reference_rows(0)

    @pl.when(r < track - 1)
    def _():
        arrive(ahead)
        window[(deep + 1) * rows :, :] = sources(ahead)[0:HALO]
        refs[HALO + rows :, :] = reference_rows(ahead)[0:HALO]

    for j in range(1, back + 1):

        @pl.when(r - j >= 0)
        def _():
            arrive(j)
            window[(deep - j) * rows : (deep - j + 1) * rows, :] = sources(j)
            if j == 1:
                refs[0:HALO, :] = reference_rows(j)[rows - HALO :]

    first_frame = lax.broadcasted_iota(jnp.int32, (span, wide), 1) < ext
    begin = deep * rows - HALO

    def one_plane(index, m, q):
        o = offs[index]
        near_rows = window[pl.ds(begin - o, span), :]
        far_rows = window[pl.ds(begin - 2 * o, span), :]
        sampled = jnp.where(first_frame, near_rows, far_rows)
        term = jnp.minimum(jnp.abs(refs[...] - sampled), CLIP)
        high = term.astype(jnp.bfloat16)
        low = (term - high.astype(jnp.float32)).astype(jnp.bfloat16)
        terms[m * span : (m + 1) * span, 2 * q * wide : (2 * q + 1) * wide] = high
        terms[m * span : (m + 1) * span, (2 * q + 1) * wide : (2 * q + 2) * wide] = low

    t_pos = r * rows + lax.broadcasted_iota(jnp.int32, (rows, lanes), 0)
    a_pos = c * cols + lax.broadcasted_iota(jnp.int32, (rows, lanes), 1) % cols

    def window_count(position, length):
        return (
            jnp.minimum(position + RADIUS, length - 1) - jnp.maximum(position - RADIUS, 0) + 1
        ).astype(jnp.float32)

    count = window_count(t_pos, track * rows) * window_count(a_pos, across * cols)
    scale = -1.0 / (SHARPNESS * count)
    has_before = jnp.where(r > 0, 1.0, 0.0)
    has_after = jnp.where(r < track - 1, 1.0, 0.0)
    top[...] = jnp.full((rows, lanes), -jnp.inf, jnp.float32)

    def batch_step(b, carry):
        for m in range(BATCH):
            for q in range(GROUP):
                one_plane(b * (BATCH * GROUP) + m * GROUP + q, m, q)
        summed = jnp.dot(terms[...], weights[...], preferred_element_type=jnp.float32)
        for m in range(BATCH):
            y = summed[m * span : (m + 1) * span]
            y = jnp.concatenate(
                [y[:HALO] * has_before, y[HALO : HALO + rows], y[HALO + rows :] * has_after], axis=0
            )
            total = y
            for k, step in enumerate((1, 2, 4)):
                box[m, k, 0:span, :] = total
                total = total + box[m, k, step : step + span, :]
            total = total[: span - 8] + total[8:]
            total = total[:rows] + total[HALO : HALO + rows] - y[:rows]
            score = total * scale
            scores[b * BATCH + m] = score
            top[...] = jnp.maximum(top[...], score)
        return carry

    lax.fori_loop(0, planes // (BATCH * GROUP), batch_step, 0)

    def over_blocks(x, op):
        step = cols
        while step < lanes:
            x = op(x, pltpu.roll(x, step, 1))
            step *= 2
        return x

    peak = over_blocks(top[...], jnp.maximum)
    block_of = lax.broadcasted_iota(jnp.int32, (1, lanes), 1) // cols
    part = 32
    masses, moments = [], []
    for lo in range(0, rows, part):
        high = peak[lo : lo + part]

        def gather(g, carry):
            mass, moment = carry
            value = jnp.zeros((1, lanes), jnp.float32)
            for q in range(GROUP):
                value = jnp.where(block_of == q, offs[g * GROUP + q].astype(jnp.float32), value)
            lifted = jnp.exp(scores[g, lo : lo + part, :] - high)
            return mass + lifted, moment + lifted * value

        zero = jnp.zeros((part, lanes), jnp.float32)
        mass, moment = lax.fori_loop(0, planes // GROUP, gather, (zero, zero), unroll=4)
        masses.append(mass)
        moments.append(moment)
    mass = over_blocks(jnp.concatenate(masses, axis=0), jnp.add)
    moment = over_blocks(jnp.concatenate(moments, axis=0), jnp.add)
    own = [x.T[0:cols] for x in (peak, mass, moment)]
    for k in range(3):
        tx[k] = own[k]

    def merge_copy(i):
        return pltpu.make_async_remote_copy(
            src_ref=tx,
            dst_ref=mrx.at[i - 1],
            send_sem=msend.at[i - 1],
            recv_sem=mrecv.at[i - 1],
            device_id={"disp": lax.rem(d + i, disp)},
        )

    for i in range(1, disp):
        merge_copy(i).start()
    for slot in range(back + 2):
        for dc, imgs in each_copy(slot):

            @pl.when(present(shift_of(slot), dc))
            def _():
                for image in imgs:
                    copy(slot, image, dc).wait_send()

    peak, mass, moment = own
    for i in range(1, disp):
        merge_copy(i).wait_recv()
        other = [mrx[i - 1, k] for k in range(3)]
        new = jnp.maximum(peak, other[0])
        mine, theirs = jnp.exp(peak - new), jnp.exp(other[0] - new)
        mass = mass * mine + other[1] * theirs
        moment = moment * mine + other[2] * theirs
        peak = new
    disp_out[...] = moment / mass / INTERVAL
    soft_out[...] = -SHARPNESS * (peak + jnp.log(mass))
    for i in range(1, disp):
        merge_copy(i).wait_send()


def shards(track, across, disp, ref_image, source_one, source_two, plane_offsets, intersection_mask):
    cols, rows = ref_image.shape
    planes = plane_offsets.shape[0]
    ext = cols + 2 * HALO
    wide, span, lanes = 2 * ext, rows + 2 * HALO, GROUP * cols
    deep = -(-(2 * (MAXD - 1) + RADIUS) // rows)
    back = min(deep, track - 1)
    vmem = pl.BlockSpec(memory_space=pltpu.VMEM)
    smem = pl.BlockSpec(memory_space=pltpu.SMEM)
    out = jax.ShapeDtypeStruct((cols, rows), jnp.float32)
    return pl.pallas_call(
        functools.partial(kernel, (track, across, disp, cols, rows, planes)),
        out_shape=(out, out),
        in_specs=[smem, smem, vmem, vmem, vmem],
        out_specs=(vmem, vmem),
        scratch_shapes=[
            pltpu.VMEM((back + 2, 3, ext, rows), jnp.bfloat16),
            pltpu.VMEM(((deep + 1) * rows + HALO, wide), jnp.float32),
            pltpu.VMEM((span, wide), jnp.float32),
            pltpu.VMEM((2 * GROUP * wide, lanes), jnp.bfloat16),
            pltpu.VMEM((BATCH * span, 2 * GROUP * wide), jnp.bfloat16),
            pltpu.VMEM((BATCH, 3, span + 8, lanes), jnp.float32),
            pltpu.VMEM((planes // GROUP, rows, lanes), jnp.float32),
            pltpu.VMEM((rows, lanes), jnp.float32),
            pltpu.VMEM((3, cols, rows), jnp.float32),
            pltpu.VMEM((max(disp - 1, 1), 3, cols, rows), jnp.float32),
            pltpu.SemaphoreType.DMA((back + 2, 3, 3)),
            pltpu.SemaphoreType.DMA((back + 2, 3, 3)),
            pltpu.SemaphoreType.DMA((max(disp - 1, 1),)),
            pltpu.SemaphoreType.DMA((max(disp - 1, 1),)),
        ],
        compiler_params=pltpu.CompilerParams(collective_id=0, has_side_effects=True),
    )(plane_offsets, intersection_mask, ref_image, source_one, source_two)


def solution(mesh):
    sizes = (mesh.shape["track"], mesh.shape["across"], mesh.shape["disp"])
    tiles = P(("groups", "across"), "track")
    return jax.shard_map(
        functools.partial(shards, *sizes),
        mesh=mesh,
        in_specs=(tiles, tiles, tiles, P("disp"), P(None, ("groups", "across"), "track")),
        out_specs=(tiles, tiles),
        check_vma=False,
    )
```

```python
import functools

import jax
import jax.numpy as jnp
from jax import lax
from jax.experimental import pallas as pl
from jax.experimental.pallas import tpu as pltpu
from jax.sharding import PartitionSpec as P

MAXD = 320
RADIUS = 15
HALO = RADIUS + 1
CLIP = 2.0
SHARPNESS = 0.005
INTERVAL = 64.0
BIG = 1e30
GROUP = 4
BATCH = 4


def kernel(
    sizes, offs_hbm, mask_hbm, r_ref, s1_ref, s2_ref, out,
    offs, mask, rx, window0, window1, refs0, refs1, weights, terms_even, terms_odd, box, scores, scales, top, tx, mrx,
    send_sem, recv_sem, msend, mrecv, local_sem,
):
    track, across, disp, cols, rows, planes = sizes
    ext = cols + 2 * HALO
    wide = 2 * ext
    span = rows + 2 * HALO
    deep = -(-(2 * (MAXD - 1) + RADIUS) // rows)
    deep0 = -(-(MAXD - 1 + RADIUS) // rows)
    back = min(deep, track - 1)
    ahead = back + 1
    r = lax.axis_index("track")
    c = lax.axis_index("across")
    d = lax.axis_index("disp")
    images = (s1_ref, s2_ref, r_ref)

    def present(dr, dc):
        return (r + dr >= 0) & (r + dr < track) & (c + dc >= 0) & (c + dc < across)

    barrier = pltpu.get_barrier_semaphore()
    for dr in range(-back, back + 1):
        for dc in (-1, 0, 1):
            if dr == 0 and dc == 0:
                continue

            @pl.when(present(dr, dc))
            def _():
                pl.semaphore_signal(barrier, inc=1, device_id={"track": r + dr, "across": c + dc})

    for i in range(1, disp):
        pl.semaphore_signal(barrier, inc=1, device_id={"disp": lax.rem(d + i, disp)})
    local = [
        pltpu.make_async_copy(offs_hbm, offs, local_sem.at[3]),
        pltpu.make_async_copy(mask_hbm, mask, local_sem.at[4]),
    ] + [
        pltpu.make_async_copy(images[i], rx.at[0, i, pl.ds(HALO, cols)], local_sem.at[i]) for i in range(3)
    ]
    for one in local:
        one.start()
    n_rows = jnp.minimum(r, back) + jnp.minimum(track - 1 - r, back) + 1
    n_cols = jnp.minimum(c, 1) + jnp.minimum(across - 1 - c, 1) + 1
    def needed(slot):
        if slot == ahead:
            return (0, 1, 2)
        if slot <= 1:
            return (0, 1, 2)
        return (0, 1) if slot <= deep0 else (1,)

    def shift_of(slot):
        return -1 if slot == ahead else slot

    def copy(slot, image, dc):
        if dc == 0:
            src, lo, n = images[image], HALO, cols
        elif dc == 1:
            src, lo, n = images[image].at[pl.ds(cols - HALO, HALO)], 0, HALO
        else:
            src, lo, n = images[image].at[pl.ds(0, HALO)], HALO + cols, HALO
        return pltpu.make_async_remote_copy(
            src_ref=src,
            dst_ref=rx.at[slot, image, pl.ds(lo, n)],
            send_sem=send_sem.at[slot, image, dc + 1],
            recv_sem=recv_sem.at[slot, image, dc + 1],
            device_id={"track": r + shift_of(slot), "across": c + dc},
        )

    def each_copy(slot):
        for dc in (-1, 0, 1):
            if shift_of(slot) == 0 and dc == 0:
                continue
            yield dc, needed(slot)

    for slot in range(back + 2):
        for lo, edge in ((0, c == 0), (HALO + cols, c == across - 1)):

            @pl.when(edge)
            def _():
                for i in range(3):
                    rx[slot, i, lo : lo + HALO, :] = jnp.zeros((HALO, rows), jnp.bfloat16)

    for j in range(1, deep + 1):

        @pl.when(r - j < 0)
        def _():
            for window in (window0, window1):
                window[(deep - j) * rows : (deep - j + 1) * rows, :] = jnp.full((rows, wide), BIG, jnp.float32)

    for slot in range(deep0 + 1, back + 1):
        rx[slot, 0] = jnp.zeros((ext, rows), jnp.bfloat16)

    @pl.when(r == 0)
    def _():
        for refs in (refs0, refs1):
            refs[0:HALO, :] = jnp.zeros((HALO, wide), jnp.float32)

    @pl.when(r == track - 1)
    def _():
        for refs, window in ((refs0, window0), (refs1, window1)):
            refs[HALO + rows :, :] = jnp.zeros((HALO, wide), jnp.float32)
            window[(deep + 1) * rows :, :] = jnp.zeros((HALO, wide), jnp.float32)

    lanes = GROUP * cols
    k_lane = lax.broadcasted_iota(jnp.int32, (wide, lanes), 0)
    n_lane = lax.broadcasted_iota(jnp.int32, (wide, lanes), 1)
    column = k_lane % ext - HALO
    gcol = column + c * cols
    near = (
        (jnp.abs(column - n_lane % cols) <= RADIUS) & (gcol >= 0) & (gcol < across * cols)
    )
    for p in range(GROUP // 2):
        hit = near & (n_lane // cols == 2 * p + k_lane // ext)
        part = jnp.where(hit, 1.0, 0.0).astype(jnp.bfloat16)
        for half in range(2):
            lo = (2 * p + half) * wide
            weights[lo : lo + wide, :] = part

    t_pos = r * rows + lax.broadcasted_iota(jnp.int32, (rows, lanes), 0)
    a_pos = c * cols + lax.broadcasted_iota(jnp.int32, (rows, lanes), 1) % cols

    def window_count(position, length):
        return (
            jnp.minimum(position + RADIUS, length - 1) - jnp.maximum(position - RADIUS, 0) + 1
        ).astype(jnp.float32)

    count = window_count(t_pos, track * rows) * window_count(a_pos, across * cols)
    scales[...] = -1.0 / (SHARPNESS * count)
    has_before = jnp.where(r > 0, 1.0, 0.0)
    has_after = jnp.where(r < track - 1, 1.0, 0.0)
    top[...] = jnp.full((rows, lanes), -jnp.inf, jnp.float32)

    pl.semaphore_wait(barrier, n_rows * n_cols - 1 + disp - 1)

    for slot in list(range(back, -1, -1)) + [ahead]:
        for dc, imgs in each_copy(slot):

            @pl.when(present(shift_of(slot), dc))
            def _():
                for image in imgs:
                    copy(slot, image, dc).start()

    for one in local:
        one.wait()
    w0 = mask[0, 0, 0].astype(jnp.float32)
    w1 = mask[0, 0, 1].astype(jnp.float32)
    share = jnp.where(w0 + w1 > 1.5, 0.5, 1.0)
    w0, w1 = w0 * share, w1 * share

    def arrive(slot):
        for dc, imgs in each_copy(slot):

            @pl.when(present(-shift_of(slot), -dc))
            def _():
                for image in imgs:
                    copy(slot, image, dc).wait_recv()

    first_half = lax.broadcasted_iota(jnp.int32, (1, wide), 1) < ext

    def place_sources(slot, lo, n):
        both = rx[slot, 0:2].reshape(wide, rows).astype(jnp.float32).T[0:n]
        swapped = pltpu.roll(both, ext, 1)
        window0[lo : lo + n, :] = jnp.where(first_half, both, swapped) * w0
        window1[lo : lo + n, :] = jnp.where(first_half, swapped, both) * w1

    def place_reference(slot, lo, start, n):
        one = rx[slot, 2].astype(jnp.float32)
        both = jnp.concatenate([one, one], axis=0).T[start : start + n]
        refs0[lo : lo + n, :] = both * w0
        refs1[lo : lo + n, :] = both * w1

    arrive(0)
    place_sources(0, deep * rows, rows)
    place_reference(0, HALO, 0, rows)

    @pl.when(r < track - 1)
    def _():
        arrive(ahead)
        place_sources(ahead, (deep + 1) * rows, HALO)
        place_reference(ahead, HALO + rows, 0, HALO)

    for j in range(1, back + 1):

        @pl.when(r - j >= 0)
        def _():
            arrive(j)
            place_sources(j, (deep - j) * rows, rows)
            if j == 1:
                place_reference(j, 0, rows - HALO, HALO)

    first = lax.broadcasted_iota(jnp.int32, (span, wide), 1) < ext
    begin = deep * rows - HALO
    clip0, clip1 = CLIP * w0, CLIP * w1

    def one_pair(index, terms, m, p):
        o, q = offs[index], offs[index + 1]

        def part(window, refs, clip, times):
            sampled = jnp.where(
                first, window[pl.ds(begin - times * o, span), :], window[pl.ds(begin - times * q, span), :]
            )
            return jnp.minimum(jnp.abs(refs[...] - sampled), clip)

        term = part(window0, refs0, clip0, 1) + part(window1, refs1, clip1, 2)
        high = term.astype(jnp.bfloat16)
        low = (term - high.astype(jnp.float32)).astype(jnp.bfloat16)
        terms[m * span : (m + 1) * span, 2 * p * wide : (2 * p + 1) * wide] = high
        terms[m * span : (m + 1) * span, (2 * p + 1) * wide : (2 * p + 2) * wide] = low

    def fill(b, terms):
        for m in range(BATCH):
            for p in range(GROUP // 2):
                one_pair(b * (BATCH * GROUP) + m * GROUP + 2 * p, terms, m, p)

    def multiply(terms):
        return jnp.dot(terms[...], weights[...], preferred_element_type=jnp.float32)

    def finish(b, summed):
        for m in range(BATCH):
            y = summed[m * span : (m + 1) * span]
            y = jnp.concatenate(
                [y[:HALO] * has_before, y[HALO : HALO + rows], y[HALO + rows :] * has_after], axis=0
            )
            total = y
            for k, step in enumerate((1, 2, 4)):
                box[m, k, 0:span, :] = total
                total = total + box[m, k, step : step + span, :]
            total = total[: span - 8] + total[8:]
            total = total[:rows] + total[HALO : HALO + rows] - y[:rows]
            score = total * scales[...]
            scores[b * BATCH + m] = score
            top[...] = jnp.maximum(top[...], score)

    batches = planes // (BATCH * GROUP)

    def two_batches(i, carry):
        summed = multiply(terms_even)
        fill(2 * i + 1, terms_odd)
        finish(2 * i, summed)
        summed = multiply(terms_odd)
        fill(2 * i + 2, terms_even)
        finish(2 * i + 1, summed)
        return carry

    fill(0, terms_even)
    lax.fori_loop(0, batches // 2 - 1, two_batches, 0)
    summed = multiply(terms_even)
    fill(batches - 1, terms_odd)
    finish(batches - 2, summed)
    finish(batches - 1, multiply(terms_odd))

    def over_blocks(x, op):
        step = cols
        while step < lanes:
            x = op(x, pltpu.roll(x, step, 1))
            step *= 2
        return x

    peak = over_blocks(top[...], jnp.maximum)
    block_of = lax.broadcasted_iota(jnp.int32, (1, lanes), 1) // cols
    part = 32
    masses, moments = [], []
    for lo in range(0, rows, part):
        high = peak[lo : lo + part]

        def gather(g, carry):
            mass, moment = carry
            value = jnp.zeros((1, lanes), jnp.float32)
            for q in range(GROUP):
                value = jnp.where(block_of == q, offs[g * GROUP + q].astype(jnp.float32), value)
            lifted = jnp.exp(scores[g, lo : lo + part, :] - high)
            return mass + lifted, moment + lifted * value

        zero = jnp.zeros((part, lanes), jnp.float32)
        mass, moment = lax.fori_loop(0, planes // GROUP, gather, (zero, zero), unroll=4)
        masses.append(mass)
        moments.append(moment)
    mass = over_blocks(jnp.concatenate(masses, axis=0), jnp.add)
    moment = over_blocks(jnp.concatenate(moments, axis=0), jnp.add)
    own = [x.T[0:cols] for x in (peak, mass, moment)]
    for k in range(3):
        tx[k] = own[k]

    def merge_copy(i):
        return pltpu.make_async_remote_copy(
            src_ref=tx,
            dst_ref=mrx.at[i - 1],
            send_sem=msend.at[i - 1],
            recv_sem=mrecv.at[i - 1],
            device_id={"disp": lax.rem(d + i, disp)},
        )

    for i in range(1, disp):
        merge_copy(i).start()
    for slot in range(back + 2):
        for dc, imgs in each_copy(slot):

            @pl.when(present(shift_of(slot), dc))
            def _():
                for image in imgs:
                    copy(slot, image, dc).wait_send()

    peak, mass, moment = own
    for i in range(1, disp):
        merge_copy(i).wait_recv()
        other = [mrx[i - 1, k] for k in range(3)]
        new = jnp.maximum(peak, other[0])
        mine, theirs = jnp.exp(peak - new), jnp.exp(other[0] - new)
        mass = mass * mine + other[1] * theirs
        moment = moment * mine + other[2] * theirs
        peak = new
    out[0], out[1], out[2] = peak, mass, moment
    for i in range(1, disp):
        merge_copy(i).wait_send()


def shards(track, across, disp, ref_image, source_one, source_two, plane_offsets, intersection_mask):
    cols, rows = ref_image.shape
    planes = plane_offsets.shape[0]
    ext = cols + 2 * HALO
    wide, span, lanes = 2 * ext, rows + 2 * HALO, GROUP * cols
    deep = -(-(2 * (MAXD - 1) + RADIUS) // rows)
    back = min(deep, track - 1)
    vmem = pl.BlockSpec(memory_space=pltpu.VMEM)
    anywhere = pl.BlockSpec(memory_space=pl.ANY)
    f32 = jnp.float32
    window = pltpu.VMEM(((deep + 1) * rows + HALO, wide), f32)
    refs = pltpu.VMEM((span, wide), f32)
    terms = pltpu.VMEM((BATCH * span, GROUP * wide), jnp.bfloat16)
    merged = pl.pallas_call(
        functools.partial(kernel, (track, across, disp, cols, rows, planes)),
        out_shape=jax.ShapeDtypeStruct((3, cols, rows), f32),
        in_specs=[anywhere] * 5,
        out_specs=vmem,
        scratch_shapes=[
            pltpu.SMEM((planes,), jnp.int32),
            pltpu.SMEM((1, 1, 2), jnp.int32),
            pltpu.VMEM((back + 2, 3, ext, rows), jnp.bfloat16),
            window,
            window,
            refs,
            refs,
            pltpu.VMEM((GROUP * wide, lanes), jnp.bfloat16),
            terms,
            terms,
            pltpu.VMEM((BATCH, 3, span + 8, lanes), f32),
            pltpu.VMEM((planes // GROUP, rows, lanes), f32),
            pltpu.VMEM((rows, lanes), f32),
            pltpu.VMEM((rows, lanes), f32),
            pltpu.VMEM((3, cols, rows), f32),
            pltpu.VMEM((max(disp - 1, 1), 3, cols, rows), f32),
            pltpu.SemaphoreType.DMA((back + 2, 3, 3)),
            pltpu.SemaphoreType.DMA((back + 2, 3, 3)),
            pltpu.SemaphoreType.DMA((max(disp - 1, 1),)),
            pltpu.SemaphoreType.DMA((max(disp - 1, 1),)),
            pltpu.SemaphoreType.DMA((5,)),
        ],
        compiler_params=pltpu.CompilerParams(collective_id=0, has_side_effects=True),
    )(plane_offsets, jnp.transpose(intersection_mask, (1, 2, 0)), ref_image, source_one, source_two)
    peak, mass, moment = merged[0], merged[1], merged[2]
    return moment / mass / INTERVAL, -SHARPNESS * (peak + jnp.log(mass))


def solution(mesh):
    sizes = (mesh.shape["track"], mesh.shape["across"], mesh.shape["disp"])
    tiles = P(("groups", "across"), "track")
    return jax.shard_map(
        functools.partial(shards, *sizes),
        mesh=mesh,
        in_specs=(tiles, tiles, tiles, P("disp"), P(None, ("groups", "across"), "track")),
        out_specs=(tiles, tiles),
        check_vma=False,
    )
```

```python
import functools

import jax
import jax.numpy as jnp
from jax import lax
from jax.experimental import pallas as pl
from jax.experimental.pallas import tpu as pltpu
from jax.sharding import PartitionSpec as P

MAXD = 320
RADIUS = 15
HALO = RADIUS + 1
CLIP = 2.0
SHARPNESS = 0.005
INTERVAL = 64.0
BIG = 1e30
GROUP = 4
ROUNDER = 1.5 * 2.0**16
LOG2E = 1.4426950408889634
LN2 = 0.6931471805599453
BATCH = 4


def kernel(
    sizes, offs_hbm, mask_hbm, r_ref, s1_ref, s2_ref, out,
    offs, mask, rx, window0, window1, refs0, refs1, weights, terms_even, terms_odd, box, scores, scales, top, tx, mrx,
    send_sem, recv_sem, msend, mrecv, local_sem,
):
    track, across, disp, cols, rows, planes = sizes
    ext = cols + 2 * HALO
    wide = 2 * ext
    span = rows + 2 * HALO
    deep = -(-(2 * (MAXD - 1) + RADIUS) // rows)
    deep0 = -(-(MAXD - 1 + RADIUS) // rows)
    back = min(deep, track - 1)
    ahead = back + 1
    r = lax.axis_index("track")
    c = lax.axis_index("across")
    d = lax.axis_index("disp")
    images = (s1_ref, s2_ref, r_ref)

    def at(dr, dc):
        return {"track": r + dr, "across": c + dc}

    def beside(i):
        return {"disp": lax.rem(d + i, disp)}

    def present(dr, dc):
        return (r + dr >= 0) & (r + dr < track) & (c + dc >= 0) & (c + dc < across)

    barrier = pltpu.get_barrier_semaphore()
    for dr in sorted(range(-back, back + 1), key=abs, reverse=True):
        for dc in (-1, 0, 1):
            if dr == 0 and dc == 0:
                continue

            @pl.when(present(dr, dc))
            def _():
                pl.semaphore_signal(barrier, inc=1, device_id=at(dr, dc))

    for i in range(1, disp):
        pl.semaphore_signal(barrier, inc=1, device_id=beside(i))
    local = [
        pltpu.make_async_copy(offs_hbm, offs, local_sem.at[3]),
        pltpu.make_async_copy(mask_hbm, mask, local_sem.at[4]),
    ] + [
        pltpu.make_async_copy(images[i], rx.at[0, i, pl.ds(HALO, cols)], local_sem.at[i]) for i in range(3)
    ]
    for one in local:
        one.start()
    n_rows = jnp.minimum(r, back) + jnp.minimum(track - 1 - r, back) + 1
    n_cols = jnp.minimum(c, 1) + jnp.minimum(across - 1 - c, 1) + 1
    def shift_of(slot):
        return -1 if slot == ahead else slot

    def copy(slot, dc):
        if slot <= 1 or slot == ahead:
            some = pl.ds(0, 3)
        else:
            some = pl.ds(0, 2) if slot <= deep0 else pl.ds(1, 1)
        start, lo, n = {0: (0, HALO, cols), 1: (cols - HALO, 0, HALO), -1: (0, HALO + cols, HALO)}[dc]
        return pltpu.make_async_remote_copy(
            src_ref=rx.at[0, some, pl.ds(HALO + start, n)],
            dst_ref=rx.at[slot, some, pl.ds(lo, n)],
            send_sem=send_sem.at[slot, dc + 1],
            recv_sem=recv_sem.at[slot, dc + 1],
            device_id=at(shift_of(slot), dc),
        )

    def sides(slot):
        return (-1, 1) if slot == 0 else (-1, 0, 1)

    for slot in range(back + 2):
        for lo, edge in ((0, c == 0), (HALO + cols, c == across - 1)):

            @pl.when(edge)
            def _():
                for i in range(3):
                    rx[slot, i, lo : lo + HALO, :] = jnp.zeros((HALO, rows), jnp.bfloat16)

    for j in range(1, deep + 1):

        @pl.when(r - j < 0)
        def _():
            for window in (window0, window1):
                window[(deep - j) * rows : (deep - j + 1) * rows, :] = jnp.full((rows, wide), BIG, jnp.float32)

    for slot in range(deep0 + 1, back + 1):
        rx[slot, 0] = jnp.zeros((ext, rows), jnp.bfloat16)

    @pl.when(r == 0)
    def _():
        for refs in (refs0, refs1):
            refs[0:HALO, :] = jnp.zeros((HALO, wide), jnp.float32)

    @pl.when(r == track - 1)
    def _():
        for refs, window in ((refs0, window0), (refs1, window1)):
            refs[HALO + rows :, :] = jnp.zeros((HALO, wide), jnp.float32)
            window[(deep + 1) * rows :, :] = jnp.zeros((HALO, wide), jnp.float32)

    lanes = GROUP * cols
    k_lane = lax.broadcasted_iota(jnp.int32, (wide, lanes), 0)
    n_lane = lax.broadcasted_iota(jnp.int32, (wide, lanes), 1)
    column = k_lane % ext - HALO
    gcol = column + c * cols
    near = (
        (jnp.abs(column - n_lane % cols) <= RADIUS) & (gcol >= 0) & (gcol < across * cols)
    )
    for p in range(GROUP // 2):
        hit = near & (n_lane // cols == 2 * p + k_lane // ext)
        part = jnp.where(hit, 1.0, 0.0).astype(jnp.bfloat16)
        for half in range(2):
            lo = (2 * p + half) * wide
            weights[lo : lo + wide, :] = part

    t_pos = r * rows + lax.broadcasted_iota(jnp.int32, (rows, lanes), 0)
    a_pos = c * cols + lax.broadcasted_iota(jnp.int32, (rows, lanes), 1) % cols

    def window_count(position, length):
        return (
            jnp.minimum(position + RADIUS, length - 1) - jnp.maximum(position - RADIUS, 0) + 1
        ).astype(jnp.float32)

    count = window_count(t_pos, track * rows) * window_count(a_pos, across * cols)
    scales[...] = -LOG2E / (SHARPNESS * count)
    has_before = jnp.where(r > 0, 1.0, 0.0)
    has_after = jnp.where(r < track - 1, 1.0, 0.0)
    top[...] = jnp.full((rows, lanes), -jnp.inf, jnp.float32)

    for one in local:
        one.wait()
    pl.semaphore_wait(barrier, n_rows * n_cols - 1 + disp - 1)

    for slot in list(range(back, -1, -1)) + [ahead]:
        for dc in sides(slot):

            @pl.when(present(shift_of(slot), dc))
            def _():
                copy(slot, dc).start()

    w0 = mask[0, 0, 0].astype(jnp.float32)
    w1 = mask[0, 0, 1].astype(jnp.float32)
    share = jnp.where(w0 + w1 > 1.5, 0.5, 1.0)
    w0, w1 = w0 * share, w1 * share

    def arrive(slot):
        for dc in sides(slot):

            @pl.when(present(-shift_of(slot), -dc))
            def _():
                copy(slot, dc).wait_recv()

    first_half = lax.broadcasted_iota(jnp.int32, (1, wide), 1) < ext

    def place_sources(slot, lo, n):
        both = rx[slot, 0:2].reshape(wide, rows).astype(jnp.float32).T[0:n]
        swapped = pltpu.roll(both, ext, 1)
        window0[lo : lo + n, :] = jnp.where(first_half, both, swapped) * w0
        window1[lo : lo + n, :] = jnp.where(first_half, swapped, both) * w1

    def place_reference(slot, lo, start, n):
        one = rx[slot, 2].astype(jnp.float32)
        both = jnp.concatenate([one, one], axis=0).T[start : start + n]
        refs0[lo : lo + n, :] = both * w0
        refs1[lo : lo + n, :] = both * w1

    arrive(0)
    place_sources(0, deep * rows, rows)
    place_reference(0, HALO, 0, rows)

    @pl.when(r < track - 1)
    def _():
        arrive(ahead)
        place_sources(ahead, (deep + 1) * rows, HALO)
        place_reference(ahead, HALO + rows, 0, HALO)

    for j in range(1, back + 1):

        @pl.when(r - j >= 0)
        def _():
            arrive(j)
            place_sources(j, (deep - j) * rows, rows)
            if j == 1:
                place_reference(j, 0, rows - HALO, HALO)

    first = lax.broadcasted_iota(jnp.int32, (span, wide), 1) < ext
    begin = deep * rows - HALO
    clip0, clip1 = CLIP * w0, CLIP * w1

    def one_pair(index, terms, m, p):
        o, q = offs[index], offs[index + 1]

        def part(window, refs, clip, times):
            sampled = jnp.where(
                first, window[pl.ds(begin - times * o, span), :], window[pl.ds(begin - times * q, span), :]
            )
            return jnp.minimum(jnp.abs(refs[...] - sampled), clip)

        term = part(window0, refs0, clip0, 1) + part(window1, refs1, clip1, 2)
        high = (term + ROUNDER) - ROUNDER
        here = slice(m * span, (m + 1) * span)
        terms[here, 2 * p * wide : (2 * p + 1) * wide] = high.astype(jnp.bfloat16)
        terms[here, (2 * p + 1) * wide : (2 * p + 2) * wide] = (term - high).astype(jnp.bfloat16)

    def fill(b, terms):
        for m in range(BATCH):
            for p in range(GROUP // 2):
                one_pair(b * (BATCH * GROUP) + m * GROUP + 2 * p, terms, m, p)

    def multiply(terms):
        return jnp.dot(terms[...], weights[...], preferred_element_type=jnp.float32)

    def finish(b, summed):
        for m in range(BATCH):
            y = summed[m * span : (m + 1) * span]
            y = jnp.concatenate(
                [y[:HALO] * has_before, y[HALO : HALO + rows], y[HALO + rows :] * has_after], axis=0
            )
            total = y
            for k, step in enumerate((1, 2, 4)):
                box[m, k, 0:span, :] = total
                total = total + box[m, k, step : step + span, :]
            total = total[: span - 8] + total[8:]
            total = total[:rows] + total[HALO : HALO + rows] - y[:rows]
            score = total * scales[...]
            scores[b * BATCH + m] = score
            top[...] = jnp.maximum(top[...], score)

    batches = planes // (BATCH * GROUP)

    def two_batches(i, carry):
        summed = multiply(terms_even)
        fill(2 * i + 1, terms_odd)
        finish(2 * i, summed)
        summed = multiply(terms_odd)
        fill(2 * i + 2, terms_even)
        finish(2 * i + 1, summed)
        return carry

    fill(0, terms_even)
    lax.fori_loop(0, batches // 2 - 1, two_batches, 0)
    summed = multiply(terms_even)
    fill(batches - 1, terms_odd)
    finish(batches - 2, summed)
    finish(batches - 1, multiply(terms_odd))

    def over_blocks(x, op):
        step = cols
        while step < lanes:
            x = op(x, pltpu.roll(x, step, 1))
            step *= 2
        return x

    peak = over_blocks(top[...], jnp.maximum)
    block_of = lax.broadcasted_iota(jnp.int32, (1, lanes), 1) // cols
    part = min(64, rows)
    masses, moments = [], []
    for lo in range(0, rows, part):
        high = peak[lo : lo + part]

        def gather(g, carry):
            mass, moment = carry
            value = jnp.zeros((1, lanes), jnp.float32)
            for q in range(GROUP):
                value = jnp.where(block_of == q, offs[g * GROUP + q].astype(jnp.float32), value)
            lifted = jnp.exp2(scores[g, lo : lo + part, :] - high)
            return mass + lifted, moment + lifted * value

        zero = jnp.zeros((part, lanes), jnp.float32)
        mass, moment = lax.fori_loop(0, planes // GROUP, gather, (zero, zero), unroll=4)
        masses.append(mass)
        moments.append(moment)
    mass = over_blocks(jnp.concatenate(masses, axis=0), jnp.add)
    moment = over_blocks(jnp.concatenate(moments, axis=0), jnp.add)
    own = [x.T[0:cols] for x in (peak, mass, moment)]
    for k in range(3):
        tx[k] = own[k]

    def merge_copy(i):
        return pltpu.make_async_remote_copy(
            src_ref=tx,
            dst_ref=mrx.at[i - 1],
            send_sem=msend.at[i - 1],
            recv_sem=mrecv.at[i - 1],
            device_id=beside(i),
        )

    for i in range(1, disp):
        merge_copy(i).start()
    for slot in range(back + 2):
        for dc in sides(slot):

            @pl.when(present(shift_of(slot), dc))
            def _():
                copy(slot, dc).wait_send()

    peak, mass, moment = own
    for i in range(1, disp):
        merge_copy(i).wait_recv()
        other = [mrx[i - 1, k] for k in range(3)]
        new = jnp.maximum(peak, other[0])
        mine, theirs = jnp.exp2(peak - new), jnp.exp2(other[0] - new)
        mass = mass * mine + other[1] * theirs
        moment = moment * mine + other[2] * theirs
        peak = new
    out[0], out[1], out[2] = peak, mass, moment
    for i in range(1, disp):
        merge_copy(i).wait_send()


def shards(track, across, disp, ref_image, source_one, source_two, plane_offsets, intersection_mask):
    cols, rows = ref_image.shape
    planes = plane_offsets.shape[0]
    ext = cols + 2 * HALO
    wide, span, lanes = 2 * ext, rows + 2 * HALO, GROUP * cols
    deep = -(-(2 * (MAXD - 1) + RADIUS) // rows)
    back = min(deep, track - 1)
    vmem = pl.BlockSpec(memory_space=pltpu.VMEM)
    anywhere = pl.BlockSpec(memory_space=pl.ANY)
    f32 = jnp.float32
    window = pltpu.VMEM(((deep + 1) * rows + HALO, wide), f32)
    refs = pltpu.VMEM((span, wide), f32)
    terms = pltpu.VMEM((BATCH * span, GROUP * wide), jnp.bfloat16)
    merged = pl.pallas_call(
        functools.partial(kernel, (track, across, disp, cols, rows, planes)),
        out_shape=jax.ShapeDtypeStruct((3, cols, rows), f32),
        in_specs=[anywhere] * 5,
        out_specs=vmem,
        scratch_shapes=[
            pltpu.SMEM((planes,), jnp.int32),
            pltpu.SMEM((1, 1, 2), jnp.int32),
            pltpu.VMEM((back + 2, 3, ext, rows), jnp.bfloat16),
            window,
            window,
            refs,
            refs,
            pltpu.VMEM((GROUP * wide, lanes), jnp.bfloat16),
            terms,
            terms,
            pltpu.VMEM((BATCH, 3, span + 8, lanes), f32),
            pltpu.VMEM((planes // GROUP, rows, lanes), f32),
            pltpu.VMEM((rows, lanes), f32),
            pltpu.VMEM((rows, lanes), f32),
            pltpu.VMEM((3, cols, rows), f32),
            pltpu.VMEM((max(disp - 1, 1), 3, cols, rows), f32),
            pltpu.SemaphoreType.DMA((back + 2, 3)),
            pltpu.SemaphoreType.DMA((back + 2, 3)),
            pltpu.SemaphoreType.DMA((max(disp - 1, 1),)),
            pltpu.SemaphoreType.DMA((max(disp - 1, 1),)),
            pltpu.SemaphoreType.DMA((5,)),
        ],
        compiler_params=pltpu.CompilerParams(collective_id=0, has_side_effects=True),
    )(plane_offsets, jnp.transpose(intersection_mask, (1, 2, 0)), ref_image, source_one, source_two)
    peak, mass, moment = merged[0], merged[1], merged[2]
    return moment / mass / INTERVAL, -SHARPNESS * (peak * LN2 + jnp.log(mass))


def solution(mesh):
    sizes = (mesh.shape["track"], mesh.shape["across"], mesh.shape["disp"])
    tiles = P(("groups", "across"), "track")
    return jax.shard_map(
        functools.partial(shards, *sizes),
        mesh=mesh,
        in_specs=(tiles, tiles, tiles, P("disp"), P(None, ("groups", "across"), "track")),
        out_specs=(tiles, tiles),
        check_vma=False,
    )
```

```python
import functools

import jax
import jax.numpy as jnp
from jax import lax
from jax.experimental import pallas as pl
from jax.experimental.pallas import tpu as pltpu
from jax.sharding import PartitionSpec as P

MAXD = 320
RADIUS = 15
HALO = RADIUS + 1
CLIP = 2.0
SHARPNESS = 0.005
INTERVAL = 64.0
BIG = 1e30
GROUP = 4
LOG2E = 1.4426950408889634
LN2 = 0.6931471805599453
BATCH = 4


def kernel(
    sizes, offs_hbm, mask_hbm, r_ref, s1_ref, s2_ref, out,
    offs, mask, rx, window0, window1, refs0, refs1, weights, terms_even, terms_odd, box, scores, scales, top, tx, mrx,
    send_sem, recv_sem, msend, mrecv, local_sem,
):
    track, across, disp, cols, rows, planes = sizes
    ext = cols + 2 * HALO
    wide = 2 * ext
    span = rows + 2 * HALO
    deep = -(-(2 * (MAXD - 1) + RADIUS) // rows)
    deep0 = -(-(MAXD - 1 + RADIUS) // rows)
    back = min(deep, track - 1)
    ahead = back + 1
    r = lax.axis_index("track")
    c = lax.axis_index("across")
    d = lax.axis_index("disp")
    images = (s1_ref, s2_ref, r_ref)

    def at(dr, dc):
        return {"track": r + dr, "across": c + dc}

    def beside(i):
        return {"disp": lax.rem(d + i, disp)}

    def present(dr, dc):
        return (r + dr >= 0) & (r + dr < track) & (c + dc >= 0) & (c + dc < across)

    barrier = pltpu.get_barrier_semaphore()
    for dr in range(-back, 2):
        for dc in (-1, 0, 1):
            if dr == 0 and dc == 0:
                continue

            @pl.when(present(dr, dc))
            def _():
                pl.semaphore_signal(barrier, inc=1, device_id=at(dr, dc))

    for i in range(1, disp):
        pl.semaphore_signal(barrier, inc=1, device_id=beside(i))
    local = [
        pltpu.make_async_copy(offs_hbm, offs, local_sem.at[3]),
        pltpu.make_async_copy(mask_hbm, mask, local_sem.at[4]),
    ] + [
        pltpu.make_async_copy(images[i], rx.at[0, i, pl.ds(HALO, cols)], local_sem.at[i]) for i in range(3)
    ]
    for one in local:
        one.start()
    n_rows = jnp.minimum(r, 1) + jnp.minimum(track - 1 - r, back) + 1
    n_cols = jnp.minimum(c, 1) + jnp.minimum(across - 1 - c, 1) + 1
    def shift_of(slot):
        return -1 if slot == ahead else slot

    def copy(slot, dc):
        if slot <= 1 or slot == ahead:
            some = pl.ds(0, 3)
        else:
            some = pl.ds(0, 2) if slot <= deep0 else pl.ds(1, 1)
        start, lo, n = {0: (0, HALO, cols), 1: (cols - HALO, 0, HALO), -1: (0, HALO + cols, HALO)}[dc]
        return pltpu.make_async_remote_copy(
            src_ref=rx.at[0, some, pl.ds(HALO + start, n)],
            dst_ref=rx.at[slot, some, pl.ds(lo, n)],
            send_sem=send_sem.at[slot, dc + 1],
            recv_sem=recv_sem.at[slot, dc + 1],
            device_id=at(shift_of(slot), dc),
        )

    def sides(slot):
        return (-1, 1) if slot == 0 else (-1, 0, 1)

    for slot in range(back + 2):
        for lo, edge in ((0, c == 0), (HALO + cols, c == across - 1)):

            @pl.when(edge)
            def _():
                for i in range(3):
                    rx[slot, i, lo : lo + HALO, :] = jnp.zeros((HALO, rows), jnp.bfloat16)

    for j in range(1, deep + 1):

        @pl.when(r - j < 0)
        def _():
            for window in (window0, window1):
                window[(deep - j) * rows : (deep - j + 1) * rows, :] = jnp.full((rows, wide), BIG, jnp.float32)

    for slot in range(deep0 + 1, back + 1):
        rx[slot, 0] = jnp.zeros((ext, rows), jnp.bfloat16)

    @pl.when(r == 0)
    def _():
        for refs in (refs0, refs1):
            refs[0:HALO, :] = jnp.zeros((HALO, wide), jnp.float32)

    @pl.when(r == track - 1)
    def _():
        for refs, window in ((refs0, window0), (refs1, window1)):
            refs[HALO + rows :, :] = jnp.zeros((HALO, wide), jnp.float32)
            window[(deep + 1) * rows :, :] = jnp.zeros((HALO, wide), jnp.float32)

    lanes = GROUP * cols
    k_lane = lax.broadcasted_iota(jnp.int32, (wide, lanes), 0)
    n_lane = lax.broadcasted_iota(jnp.int32, (wide, lanes), 1)
    column = k_lane % ext - HALO
    gcol = column + c * cols
    near = (
        (jnp.abs(column - n_lane % cols) <= RADIUS) & (gcol >= 0) & (gcol < across * cols)
    )
    for p in range(GROUP // 2):
        hit = near & (n_lane // cols == 2 * p + k_lane // ext)
        part = jnp.where(hit, 1.0, 0.0).astype(jnp.bfloat16)
        for half in range(2):
            lo = (2 * p + half) * wide
            weights[lo : lo + wide, :] = part

    t_pos = r * rows + lax.broadcasted_iota(jnp.int32, (rows, lanes), 0)
    a_pos = c * cols + lax.broadcasted_iota(jnp.int32, (rows, lanes), 1) % cols

    def window_count(position, length):
        return (
            jnp.minimum(position + RADIUS, length - 1) - jnp.maximum(position - RADIUS, 0) + 1
        ).astype(jnp.float32)

    count = window_count(t_pos, track * rows) * window_count(a_pos, across * cols)
    scales[...] = -LOG2E / (SHARPNESS * count)
    has_before = jnp.where(r > 0, 1.0, 0.0)
    has_after = jnp.where(r < track - 1, 1.0, 0.0)
    top[...] = jnp.full((rows, lanes), -jnp.inf, jnp.float32)

    for one in local:
        one.wait()
    pl.semaphore_wait(barrier, n_rows * n_cols - 1 + disp - 1)

    for slot in list(range(back, -1, -1)) + [ahead]:
        for dc in sides(slot):

            @pl.when(present(shift_of(slot), dc))
            def _():
                copy(slot, dc).start()

    w0 = mask[0, 0, 0].astype(jnp.float32)
    w1 = mask[0, 0, 1].astype(jnp.float32)
    share = jnp.where(w0 + w1 > 1.5, 0.5, 1.0)
    w0, w1 = w0 * share, w1 * share

    def arrive(slot):
        for dc in sides(slot):

            @pl.when(present(-shift_of(slot), -dc))
            def _():
                copy(slot, dc).wait_recv()

    first_half = lax.broadcasted_iota(jnp.int32, (1, wide), 1) < ext

    def place_sources(slot, lo, n):
        both = rx[slot, 0:2].reshape(wide, rows).astype(jnp.float32).T[0:n]
        swapped = pltpu.roll(both, ext, 1)
        window0[lo : lo + n, :] = jnp.where(first_half, both, swapped) * w0
        window1[lo : lo + n, :] = jnp.where(first_half, swapped, both) * w1

    def place_reference(slot, lo, start, n):
        one = rx[slot, 2].astype(jnp.float32)
        both = jnp.concatenate([one, one], axis=0).T[start : start + n]
        refs0[lo : lo + n, :] = both * w0
        refs1[lo : lo + n, :] = both * w1

    arrive(0)
    place_sources(0, deep * rows, rows)
    place_reference(0, HALO, 0, rows)

    @pl.when(r < track - 1)
    def _():
        arrive(ahead)
        place_sources(ahead, (deep + 1) * rows, HALO)
        place_reference(ahead, HALO + rows, 0, HALO)

    for j in range(1, back + 1):

        @pl.when(r - j >= 0)
        def _():
            arrive(j)
            place_sources(j, (deep - j) * rows, rows)
            if j == 1:
                place_reference(j, 0, rows - HALO, HALO)

    first = lax.broadcasted_iota(jnp.int32, (span, wide), 1) < ext
    begin = deep * rows - HALO
    clip0, clip1 = CLIP * w0, CLIP * w1

    def one_pair(index, terms, m, p):
        o, q = offs[index], offs[index + 1]

        def part(window, refs, clip, times):
            sampled = jnp.where(
                first, window[pl.ds(begin - times * o, span), :], window[pl.ds(begin - times * q, span), :]
            )
            return jnp.minimum(jnp.abs(refs[...] - sampled), clip)

        term = part(window0, refs0, clip0, 1) + part(window1, refs1, clip1, 2)
        high = term.astype(jnp.bfloat16)
        here = slice(m * span, (m + 1) * span)
        terms[here, 2 * p * wide : (2 * p + 1) * wide] = high
        terms[here, (2 * p + 1) * wide : (2 * p + 2) * wide] = (term - high.astype(jnp.float32)).astype(jnp.bfloat16)

    def fill(b, terms):
        for m in range(BATCH):
            for p in range(GROUP // 2):
                one_pair(b * (BATCH * GROUP) + m * GROUP + 2 * p, terms, m, p)

    def multiply(terms):
        return jnp.dot(terms[...], weights[...], preferred_element_type=jnp.float32)

    def finish(b, summed):
        for m in range(BATCH):
            y = summed[m * span : (m + 1) * span]
            y = jnp.concatenate(
                [y[:HALO] * has_before, y[HALO : HALO + rows], y[HALO + rows :] * has_after], axis=0
            )
            total = y
            for k, step in enumerate((1, 2, 4)):
                box[m, k, 0:span, :] = total
                total = total + box[m, k, step : step + span, :]
            total = total[: span - 8] + total[8:]
            total = total[:rows] + total[HALO : HALO + rows] - y[:rows]
            score = total * scales[...]
            scores[b * BATCH + m] = score
            top[...] = jnp.maximum(top[...], score)

    batches = planes // (BATCH * GROUP)

    def two_batches(i, carry):
        summed = multiply(terms_even)
        fill(2 * i + 1, terms_odd)
        finish(2 * i, summed)
        summed = multiply(terms_odd)
        fill(2 * i + 2, terms_even)
        finish(2 * i + 1, summed)
        return carry

    fill(0, terms_even)
    lax.fori_loop(0, batches // 2 - 1, two_batches, 0)
    summed = multiply(terms_even)
    fill(batches - 1, terms_odd)
    finish(batches - 2, summed)
    finish(batches - 1, multiply(terms_odd))

    def over_blocks(x, op):
        step = cols
        while step < lanes:
            x = op(x, pltpu.roll(x, step, 1))
            step *= 2
        return x

    peak = over_blocks(top[...], jnp.maximum)
    block_of = lax.broadcasted_iota(jnp.int32, (1, lanes), 1) // cols
    part = min(64, rows)
    masses, moments = [], []
    for lo in range(0, rows, part):
        high = peak[lo : lo + part]

        def gather(g, carry):
            mass, moment = carry
            value = jnp.zeros((1, lanes), jnp.float32)
            for q in range(GROUP):
                value = jnp.where(block_of == q, offs[g * GROUP + q].astype(jnp.float32), value)
            lifted = jnp.exp2(scores[g, lo : lo + part, :] - high)
            return mass + lifted, moment + lifted * value

        zero = jnp.zeros((part, lanes), jnp.float32)
        mass, moment = lax.fori_loop(0, planes // GROUP, gather, (zero, zero), unroll=8)
        masses.append(mass)
        moments.append(moment)
    mass = over_blocks(jnp.concatenate(masses, axis=0), jnp.add)
    moment = over_blocks(jnp.concatenate(moments, axis=0), jnp.add)
    own = [x.T[0:cols] for x in (peak, mass, moment)]
    for k in range(3):
        tx[k] = own[k]

    def merge_copy(i):
        return pltpu.make_async_remote_copy(
            src_ref=tx,
            dst_ref=mrx.at[i - 1],
            send_sem=msend.at[i - 1],
            recv_sem=mrecv.at[i - 1],
            device_id=beside(i),
        )

    for i in range(1, disp):
        merge_copy(i).start()
    for slot in range(back + 2):
        for dc in sides(slot):

            @pl.when(present(shift_of(slot), dc))
            def _():
                copy(slot, dc).wait_send()

    peak, mass, moment = own
    for i in range(1, disp):
        merge_copy(i).wait_recv()
        other = [mrx[i - 1, k] for k in range(3)]
        new = jnp.maximum(peak, other[0])
        mine, theirs = jnp.exp2(peak - new), jnp.exp2(other[0] - new)
        mass = mass * mine + other[1] * theirs
        moment = moment * mine + other[2] * theirs
        peak = new
    out[0], out[1], out[2] = peak, mass, moment
    for i in range(1, disp):
        merge_copy(i).wait_send()


def shards(track, across, disp, ref_image, source_one, source_two, plane_offsets, intersection_mask):
    cols, rows = ref_image.shape
    planes = plane_offsets.shape[0]
    ext = cols + 2 * HALO
    wide, span, lanes = 2 * ext, rows + 2 * HALO, GROUP * cols
    deep = -(-(2 * (MAXD - 1) + RADIUS) // rows)
    back = min(deep, track - 1)
    vmem = pl.BlockSpec(memory_space=pltpu.VMEM)
    anywhere = pl.BlockSpec(memory_space=pl.ANY)
    f32 = jnp.float32
    window = pltpu.VMEM(((deep + 1) * rows + HALO, wide), f32)
    refs = pltpu.VMEM((span, wide), f32)
    terms = pltpu.VMEM((BATCH * span, GROUP * wide), jnp.bfloat16)
    merged = pl.pallas_call(
        functools.partial(kernel, (track, across, disp, cols, rows, planes)),
        out_shape=jax.ShapeDtypeStruct((3, cols, rows), f32),
        in_specs=[anywhere] * 5,
        out_specs=vmem,
        scratch_shapes=[
            pltpu.SMEM((planes,), jnp.int32),
            pltpu.SMEM((1, 1, 2), jnp.int32),
            pltpu.VMEM((back + 2, 3, ext, rows), jnp.bfloat16),
            window,
            window,
            refs,
            refs,
            pltpu.VMEM((GROUP * wide, lanes), jnp.bfloat16),
            terms,
            terms,
            pltpu.VMEM((BATCH, 3, span + 8, lanes), f32),
            pltpu.VMEM((planes // GROUP, rows, lanes), f32),
            pltpu.VMEM((rows, lanes), f32),
            pltpu.VMEM((rows, lanes), f32),
            pltpu.VMEM((3, cols, rows), f32),
            pltpu.VMEM((max(disp - 1, 1), 3, cols, rows), f32),
            pltpu.SemaphoreType.DMA((back + 2, 3)),
            pltpu.SemaphoreType.DMA((back + 2, 3)),
            pltpu.SemaphoreType.DMA((max(disp - 1, 1),)),
            pltpu.SemaphoreType.DMA((max(disp - 1, 1),)),
            pltpu.SemaphoreType.DMA((5,)),
        ],
        compiler_params=pltpu.CompilerParams(collective_id=0, has_side_effects=True),
    )(plane_offsets, jnp.transpose(intersection_mask, (1, 2, 0)), ref_image, source_one, source_two)
    peak, mass, moment = merged[0], merged[1], merged[2]
    return moment / mass / INTERVAL, -SHARPNESS * (peak * LN2 + jnp.log(mass))


def solution(mesh):
    sizes = (mesh.shape["track"], mesh.shape["across"], mesh.shape["disp"])
    tiles = P(("groups", "across"), "track")
    return jax.shard_map(
        functools.partial(shards, *sizes),
        mesh=mesh,
        in_specs=(tiles, tiles, tiles, P("disp"), P(None, ("groups", "across"), "track")),
        out_specs=(tiles, tiles),
        check_vma=False,
    )
```
